256 devices in a mesh: section: 4 (over x), dp: 8 (over y, core), expert: 8 (over z).
Axes of the slice: x: 4, y: 4, z: 8, core: 2. Of those that a mesh axis runs over, the one named last changes fastest.
Arguments:
- patches: bfloat16 [32768, 1152], P(('dp', 'expert')), may hold values from -50 to 50
- lengths: int32 [64, 4], P(('dp', 'expert')), may hold values from 1 to 64, 128 in all within a row
- w_qkv: bfloat16 [1152, 3456], P(None, 'section'), may hold values from -4.714045 to 4.714045
- w_out: bfloat16 [1152, 1152], P('section'), may hold values from -0.1875 to 0.1875
- w_proj: bfloat16 [4608, 2048], P('dp', 'section'), may hold values from -0.09375 to 0.09375
- routes: int32 [8192, 6], P(('dp', 'expert')), may hold values from 0 to 63, all different within a row; in each aligned block of 128 rows (0 to 127, 128 to 255, ...) at most 24 rows name the same one
- gates: float32 [8192, 6], P(('dp', 'expert')), may hold values from 0.05 to 0.4
- w_gate: bfloat16 [64, 2048, 1408], P(('dp', 'expert'), None, 'section'), may hold values from -0.125 to 0.125
- w_up: bfloat16 [64, 2048, 1408], P(('dp', 'expert'), None, 'section'), may hold values from -0.125 to 0.125
- w_down: bfloat16 [64, 1408, 2048], P(('dp', 'expert'), 'section'), may hold values from -0.15625 to 0.15625
Outputs:
- language_out: bfloat16 [8192, 2048], P(('dp', 'expert'), 'section')
The draws below stay inside these ranges and needn't reach their ends.
Inputs may be any that keep to these rules, and one draw needn't show every extreme that they name: Each row lists, in order, the lengths in merged tokens of a group's images; they sum to 128 and the largest is exactly 64. `routes`: A token's 6 experts differ. Among the rows of one device no expert is named more than 24 times, a bound that some block reaches in every draw.
All inputs are finite; a program needn't handle non-finite values.
Results may differ from the reference program's by a relative error of at most 0.012.
Values may be sent and summed in bfloat16 or wider, within the bound.
No kernel may reach another device: no remote copies, remote signals or barrier semaphores. Data moves between devices by JAX's collectives and lax.ppermute only.
A program may use at most 64 MiB of HBM per device.

```python
import math
import jax
import jax.numpy as jnp
import numpy as np
from jax import lax

D_VIT = 1152
HEADS = 16
D_LM = 2048
FF_EXP = 1408
TOP = 6
IMAGES = 4
GROUPS = 64
EXPERTS = 64
M_DEV = 128
PATCHES = 32768
TOKENS = 8192
CAP = 24
N_SECTION = 4


def draw_patches(key, part):
    keys = jax.random.split(key, 4)
    columns = jnp.exp(jax.random.uniform(keys[0], (D_VIT,), jnp.float32) * math.log(10.0))
    offsets = jax.random.uniform(keys[2], (D_VIT,), jnp.float32, -1.0, 1.0)
    noise = jnp.clip(jax.random.normal(keys[3], (PATCHES, D_VIT), jnp.float32), -4.0, 4.0)
    row_scale = jnp.exp(jax.random.uniform(keys[1], (PATCHES, 1), jnp.float32) * math.log(10.0)) * 0.1
    return ((noise + offsets[None, :]) * columns[None, :] * row_scale).astype(jnp.bfloat16)


def draw_w_qkv(key, part):
    keys = jax.random.split(key, 1)
    head_dim = D_VIT // HEADS
    raw = jnp.clip(jax.random.normal(keys[0], (D_VIT, HEADS, 3, head_dim), jnp.float32), -4.0, 4.0)
    raw = raw * (1.0 / math.sqrt(D_VIT))
    return raw.reshape(D_VIT, 3 * D_VIT).astype(jnp.bfloat16)


def block_levels(stream_key, dims, pieces, low, top_value):
    factor_of = 1.0
    for dim, parts in pieces:
        heights = jax.random.uniform(jax.random.fold_in(jax.random.fold_in(stream_key, 6), dim), (parts,), jnp.float32, low / len(pieces), top_value / len(pieces))
        factor_of = factor_of * jnp.repeat(jnp.exp(heights), dims[dim] // parts).reshape((-1,) + (1,) * (len(dims) - 1 - dim))
    return factor_of


def split_up(amount, total, most, lean):
    portions = [(1 << 20) // math.isqrt(standing ** lean) + 1 for standing in range(2, amount + 1)]
    surplus, given = total - most - (amount - 1), [1] * (amount - 1)
    while surplus > 0:
        candidates = [i for i in range(amount - 1) if given[i] < most]
        whole, budget = sum([portions[i] for i in candidates]), surplus
        for i in candidates:
            extra = min(most - given[i], max(1, budget * portions[i] // whole), surplus)
            given[i] = given[i] + extra
            surplus = surplus - extra
    return np.array([most] + given)


def ragged(key, number_of, total, limit, lean):
    if number_of == 2:
        one = jax.random.randint(key, (), max(1, total - limit), min(limit, total - 1) + 1)
        return jnp.stack([one, total - one])
    sizes = jnp.asarray(split_up(number_of, total, limit, lean), jnp.int32)
    couples = (number_of - 1) // 2
    source_of, sink = sizes[1:1 + 2 * couples:2], sizes[2:2 + 2 * couples:2]
    room = jnp.minimum(source_of - 1, limit - sink)
    passed = jax.random.randint(jax.random.fold_in(key, 1), (couples,), 0, 1 << 20) % (room + 1)
    sizes = sizes.at[1:1 + 2 * couples:2].set(source_of - passed).at[2:2 + 2 * couples:2].set(sink + passed)
    return sizes[jax.random.permutation(jax.random.fold_in(key, 2), number_of)]


def assign_block(rng, own, number, rows, amount, top, reach, skew):
    sequence = jax.random.permutation(rng, amount)
    crowded, usual = load_shares(amount, rows * top, reach, skew, True), load_shares(amount, rows * top, reach, skew, False)
    places = jnp.arange(amount)

    def named(sizes, turn):
        used = int((sizes > 0).sum())
        fixed = max(1, used // 4)
        passed = fixed + (places - fixed + turn * (used - fixed)) % max(1, amount - fixed)
        return jnp.zeros((amount,), jnp.int32).at[sequence[jnp.where(places < fixed, places, passed)]].set(jnp.asarray(sizes, jnp.int32))

    sizes = jnp.where(number % 4 == 0, named(crowded, number // 4), named(usual, number - number // 4 - 1))
    mixed = jax.random.permutation(jax.random.fold_in(own, 3), amount)
    source_of, sink = mixed[0:amount // 2 * 2:2], mixed[1:amount // 2 * 2:2]
    margin = jnp.minimum(sizes[source_of] - 1, reach - sizes[sink]) // 2
    margin = jnp.where((source_of == sequence[0]) | (sink == sequence[0]) | (sizes[sink] == 0), 0, jnp.maximum(margin, 0))
    passed = jax.random.randint(jax.random.fold_in(own, 4), (amount // 2,), 0, 1 << 20) % (margin + 1)
    sizes = sizes.at[source_of].add(-passed).at[sink].add(passed)
    labels = jnp.searchsorted(jnp.cumsum(sizes), jnp.arange(rows * top), side="right").astype(jnp.int32)
    table = labels.reshape(top, rows).T
    table = table[jax.random.permutation(jax.random.fold_in(own, 1), rows)]
    turn = jax.random.randint(jax.random.fold_in(own, 2), (rows, 1), 0, top)
    return jnp.take_along_axis(table, (jnp.arange(top)[None, :] + turn) % top, axis=1)


def load_shares(number_of, total, reach, skew, full):
    loads = [(1 << 20) // math.isqrt(rank ** skew) + 1 for rank in range(1, number_of + 1)]
    largest = reach if full else min(reach, max(-(-total // number_of), total * loads[0] // sum(loads)))
    least = 1 if total - largest >= number_of - 1 else 0
    given, spare = [largest] + [least] * (number_of - 1), total - largest - least * (number_of - 1)
    while spare > 0:
        free = [i for i in range(1, number_of) if given[i] < largest] or [i for i in range(1, number_of) if given[i] < reach]
        pool, left = sum([loads[i] for i in free]), spare
        for i in free:
            addition = min(reach - given[i], max(1, left * loads[i] // pool), spare)
            given[i] = given[i] + addition
            spare = spare - addition
    return np.array(given)


def bell_draw(stream_key, extent, width, most, pieces=(), held_as=jnp.bfloat16):
    values = jax.random.normal(stream_key, extent, jnp.float32) * width
    if len(pieces) > 0:
        values = block_levels(stream_key, extent, pieces, -0.22, 0.18) * values
    return jnp.clip(values, min=-most, max=most).astype(held_as)


def setup_inputs(seed: int = 0) -> dict:
    arg_keys = jax.random.split(jax.random.key(seed), 11)
    patches = draw_patches(jax.random.fold_in(arg_keys[10], 71), 0)
    lengths = jax.vmap(lambda own: ragged(own, IMAGES, M_DEV, M_DEV // 2, 2))(jax.random.split(arg_keys[1], GROUPS)).reshape((GROUPS, IMAGES)).astype(jnp.int32)
    w_qkv = draw_w_qkv(jax.random.fold_in(arg_keys[10], 71), 0)
    w_out = bell_draw(arg_keys[3], (D_VIT, D_VIT), D_VIT ** -0.5, 0.1875, ((0, 4),))
    w_proj = bell_draw(arg_keys[4], (4 * D_VIT, D_LM), (4 * D_VIT) ** -0.5, 0.09375, ((0, 8), (1, 4)))
    routes_keys = jax.random.split(jax.random.fold_in(arg_keys[5], 1), TOKENS // M_DEV)
    routes_turns = jax.random.permutation(jax.random.fold_in(arg_keys[5], 3), TOKENS // M_DEV)
    routes = jax.vmap(lambda own, number: assign_block(jax.random.fold_in(arg_keys[5], 2), own, number, M_DEV, EXPERTS, TOP, CAP, 2))(routes_keys, routes_turns).reshape((TOKENS, TOP))
    gates = jnp.clip(0.05 + 0.35 * jax.random.uniform(arg_keys[6], (TOKENS, TOP), jnp.float32) ** block_levels(arg_keys[6], (TOKENS, TOP), ((0, 64),), -0.2, 0.2), 0.05, 0.4)
    w_gate = bell_draw(arg_keys[7], (EXPERTS, D_LM, FF_EXP), D_LM ** -0.5, 0.125, ((0, 64), (2, 4)))
    w_up = bell_draw(arg_keys[8], (EXPERTS, D_LM, FF_EXP), D_LM ** -0.5, 0.125, ((0, 64), (2, 4)))
    w_down = bell_draw(arg_keys[9], (EXPERTS, FF_EXP, D_LM), FF_EXP ** -0.5, 0.15625, ((0, 64), (1, 4)))
    return {"patches": patches, "lengths": lengths, "w_qkv": w_qkv, "w_out": w_out, "w_proj": w_proj, "routes": routes, "gates": gates, "w_gate": w_gate, "w_up": w_up, "w_down": w_down}


def layer_norm(values):
    center = values - lax.optimization_barrier(jnp.mean(values, axis=-1, keepdims=True))
    spread = lax.optimization_barrier(jnp.mean(center * center, axis=-1, keepdims=True))
    return center * lax.rsqrt(spread + 1e-06)

def rms_norm(values):
    return values * lax.rsqrt(lax.optimization_barrier(jnp.mean(values * values, axis=-1, keepdims=True)) + 1e-06)

def segment_of(lengths_row, patch_count):
    ends = jnp.cumsum(lengths_row).astype(jnp.int32) * 4
    places = jnp.arange(patch_count, dtype=jnp.int32)
    return lax.optimization_barrier(jnp.sum((places[:, None] >= ends[None, :]).astype(jnp.int32), axis=1))

def reference(patches, lengths, w_qkv, w_out, w_proj, routes, gates, w_gate, w_up, w_down):
    groups = lengths.shape[0]
    patch_rows = patches.shape[0] // groups
    head_dim = D_VIT // HEADS
    scale = 1.0 / math.sqrt(head_dim)

    def encode(blocks):
        inputs, lengths_row = blocks
        normed_in = layer_norm(inputs.astype(jnp.float32)).astype(jnp.bfloat16)
        packed = jnp.dot(normed_in, w_qkv, preferred_element_type=jnp.float32).astype(jnp.bfloat16)
        packed = packed.reshape(patch_rows, HEADS, 3, head_dim).astype(jnp.float32)
        query = packed[:, :, 0]
        key_part = packed[:, :, 1]
        value_part = packed[:, :, 2]
        segment = segment_of(lengths_row, patch_rows)
        same = segment[:, None] == segment[None, :]
        scores = jnp.einsum('qhd,khd->hqk', query, key_part) * scale
        scores = jnp.where(same[None], scores, -jnp.inf)
        peak = lax.optimization_barrier(jnp.max(scores, axis=-1, keepdims=True))
        weights = jnp.where(same[None], jnp.exp(scores - peak), 0.0)
        probs = (weights / lax.optimization_barrier(jnp.sum(weights, axis=-1, keepdims=True))).astype(jnp.bfloat16)
        attended = jnp.einsum('hqk,khd->qhd', probs.astype(jnp.float32), value_part).astype(jnp.bfloat16)
        mixed = jnp.dot(attended.reshape(patch_rows, D_VIT), w_out, preferred_element_type=jnp.float32)
        encoded = inputs.astype(jnp.float32) + mixed
        return encoded.reshape(patch_rows // 4, 4 * D_VIT).astype(jnp.bfloat16)
    merged = lax.map(encode, (patches.reshape(groups, patch_rows, D_VIT), lengths))
    merged = merged.reshape(-1, 4 * D_VIT)
    projected = jnp.dot(merged, w_proj, preferred_element_type=jnp.float32).astype(jnp.bfloat16)
    normed_tokens = rms_norm(projected.astype(jnp.float32)).astype(jnp.bfloat16)
    token_total = projected.shape[0]
    merged_count = token_total // groups
    route_flat = routes.reshape(groups, merged_count * TOP)
    onehot = (route_flat[:, :, None] == jnp.arange(EXPERTS, dtype=jnp.int32)[None, None, :]).astype(jnp.int32)
    ranks = jnp.cumsum(onehot, axis=1).astype(jnp.int32) - 1
    slots = lax.optimization_barrier(jnp.sum(ranks * onehot, axis=2)).astype(jnp.int32)
    group_index = jnp.arange(groups, dtype=jnp.int32)[:, None]
    owners = group_index * merged_count + jnp.arange(merged_count * TOP, dtype=jnp.int32)[None, :] // TOP
    places = group_index * CAP + slots
    table = jnp.full((EXPERTS, groups * CAP), token_total, dtype=jnp.int32).at[route_flat, places].set(owners.astype(jnp.int32))
    weight_table = jnp.zeros((EXPERTS, groups * CAP), dtype=jnp.float32).at[route_flat, places].set(gates.reshape(groups, merged_count * TOP))
    padded = jnp.concatenate([normed_tokens, jnp.zeros((1, D_LM), dtype=jnp.bfloat16)], axis=0)
    quarter = FF_EXP // N_SECTION

    def expert_step(total, expert_index):
        picked = padded[table[expert_index]]
        gate_act = jnp.dot(picked, w_gate[expert_index], preferred_element_type=jnp.float32)
        up_act = jnp.dot(picked, w_up[expert_index], preferred_element_type=jnp.float32)
        hidden = (jax.nn.silu(gate_act) * up_act).astype(jnp.bfloat16)
        result = jnp.zeros((picked.shape[0], D_LM), dtype=jnp.float32)
        for quarter_index in range(N_SECTION):
            lower = quarter_index * quarter
            piece = jnp.dot(hidden[:, lower:lower + quarter], w_down[expert_index, lower:lower + quarter], preferred_element_type=jnp.float32).astype(jnp.bfloat16)
            piece = lax.optimization_barrier(piece)
            result = result + piece.astype(jnp.float32)
        total = total.at[table[expert_index]].add(weight_table[expert_index][:, None] * result)
        return (total, None)
    start_total = jnp.zeros((token_total + 1, D_LM), dtype=jnp.float32)
    expert_sum, unused = lax.scan(expert_step, start_total, jnp.arange(EXPERTS, dtype=jnp.int32))
    return (projected.astype(jnp.float32) + expert_sum[:token_total]).astype(jnp.bfloat16)
```

```python
import math

import jax
import jax.numpy as jnp
from jax import lax
from jax.sharding import PartitionSpec as P

D_VIT = 1152
HEADS = 16
TOP = 6
BF = jnp.bfloat16
F32 = jnp.float32


def dot(a, b):
    return jnp.dot(a, b, preferred_element_type=F32)


def shift(value, axis, step):
    count = lax.axis_size(axis)
    return lax.ppermute(value, axis, [(i, (i + step) % count) for i in range(count)])


def partner(value):
    count = lax.axis_size("dp")
    return lax.ppermute(value, "dp", [(i, i ^ 1) for i in range(count)])


def layer_norm(values):
    center = values - jnp.mean(values, axis=-1, keepdims=True)
    spread = jnp.mean(center * center, axis=-1, keepdims=True)
    return center * lax.rsqrt(spread + 1e-06)


def gather_projector(w_proj):
    rows = [w_proj] + [shift(w_proj, "dp", 2 * d) for d in (1, 2, 3)]
    first = lax.axis_index("dp") % 2 == 0
    blocks = []
    for mine in rows:
        other = partner(mine)
        low = jnp.where(first, mine, other)
        high = jnp.where(first, other, mine)
        blocks.append((low, high))
    return blocks


def route_tables(routes, gates, expert_total, capacity):
    rows = routes.shape[0]
    ids = jnp.arange(expert_total, dtype=jnp.int32)
    named = routes[:, :, None] == ids[None, None, :]
    member = jnp.any(named, axis=1)
    weight = jnp.sum(jnp.where(named, gates[:, :, None], 0.0), axis=1)
    places = jnp.arange(rows, dtype=jnp.int32)
    before = (places[:, None] > places[None, :]).astype(BF)
    slot = dot(before, member.astype(BF))
    slot = jnp.where(member, slot, 255.0).astype(BF)
    lanes = jnp.arange(expert_total * capacity, dtype=jnp.int32)
    spread = (lanes[None, :] // capacity == ids[:, None]).astype(BF)
    hit = dot(slot, spread) == (lanes % capacity).astype(F32)[None, :]
    high = weight.astype(BF)
    low = (weight - high.astype(F32)).astype(BF)
    pick = hit.astype(BF)
    gate_high = jnp.where(hit, dot(high, spread), 0.0).astype(BF)
    gate_low = jnp.where(hit, dot(low, spread), 0.0).astype(BF)
    return pick, gate_high, gate_low


def per_device(patches, lengths, w_qkv, w_out, w_proj, routes, gates, w_gate, w_up, w_down):
    data_count = lax.axis_size("dp")
    owner_count = lax.axis_size("expert")
    sections = lax.axis_size("section")
    section = lax.axis_index("section")
    patch_rows, width = patches.shape
    merged_count = patch_rows // 4
    head_dim = D_VIT // HEADS
    local_heads = w_qkv.shape[1] // (3 * head_dim)
    scale = 1.0 / math.sqrt(head_dim)
    expert_total = data_count * owner_count
    capacity = max(2, min(merged_count, 2 * merged_count * TOP // expert_total))
    columns = w_proj.shape[1]

    out_rows = [w_out] + [shift(w_out, "section", d) for d in range(1, sections)]
    proj_blocks = gather_projector(w_proj)

    normed_in = layer_norm(patches.astype(F32)).astype(BF)
    packed = dot(normed_in, w_qkv).astype(BF)
    packed = packed.reshape(patch_rows, local_heads, 3, head_dim)
    query = packed[:, :, 0]
    key_part = packed[:, :, 1]
    value_part = packed[:, :, 2]
    ends = jnp.cumsum(lengths[0]) * 4
    places = jnp.arange(patch_rows, dtype=jnp.int32)
    segment = jnp.sum((places[:, None] >= ends[None, :]).astype(jnp.int32), axis=1)
    same = segment[:, None] == segment[None, :]
    scores = jnp.einsum("qhd,khd->hqk", query, key_part, preferred_element_type=F32) * scale
    scores = jnp.where(same[None], scores, -jnp.inf)
    peak = jnp.max(scores, axis=-1, keepdims=True)
    weights = jnp.where(same[None], jnp.exp(scores - peak), 0.0)
    probs = (weights / jnp.sum(weights, axis=-1, keepdims=True)).astype(BF)
    attended = jnp.einsum("hqk,khd->qhd", probs, value_part, preferred_element_type=F32)
    attended = attended.astype(BF).reshape(patch_rows, local_heads * head_dim)

    parts = [attended] + [shift(attended, "section", d) for d in range(1, sections)]
    summed = sum(dot(parts[d], out_rows[d]) for d in range(sections))
    encoded = (patches.astype(F32) + summed).astype(BF).reshape(merged_count, 4, width)
    row_y = lax.axis_index("dp") // 2
    proj = jnp.zeros((merged_count, columns), F32)
    half = w_proj.shape[0]
    for d in range(4):
        block = lax.dynamic_index_in_dim(encoded, (row_y - d) % 4, axis=1, keepdims=False)
        low, high = proj_blocks[d]
        proj = proj + dot(block[:, :half], low) + dot(block[:, half:], high)
    proj_own = proj.astype(BF)

    pick, gate_high, gate_low = route_tables(routes, gates, expert_total, capacity)
    outgoing = lax.dot_general(pick, proj_own, (((0,), (0,)), ((), ())), preferred_element_type=F32)
    outgoing = outgoing.astype(BF).reshape(expert_total, capacity, columns)
    received = lax.all_to_all(outgoing, ("dp", "expert"), split_axis=0, concat_axis=0, tiled=True)
    rows = expert_total * capacity
    own = received.reshape(rows, columns)

    split = rows // 2
    own_a, own_b = own[:split], own[split:]
    left_a = shift(own_a, "section", 1)
    right_b = shift(own_b, "section", -1)
    left_b = shift(own_b, "section", 1)
    right_a = shift(own_a, "section", -1)
    far_a = shift(left_a, "section", 1)
    far_b = shift(right_b, "section", -1)
    halves = [(own_a, left_a, right_a, far_a), (own_b, left_b, right_b, far_b)]
    origin = (0, -1, 1, 2)
    full = sections * columns

    def weight_rows(w, offset):
        return lax.dynamic_slice_in_dim(w[0], ((section + offset) % sections) * columns, columns, axis=0)

    gate_w = [weight_rows(w_gate, o) for o in origin]
    up_w = [weight_rows(w_up, o) for o in origin]
    down_w = [
        lax.dynamic_slice_in_dim(w_down[0], ((section + o) % sections) * columns, columns, axis=1)
        for o in range(sections)
    ]

    results = []
    for pieces in halves:
        square = sum(
            jnp.sum(p.astype(F32) * p.astype(F32), axis=-1, keepdims=True) for p in pieces
        )
        row_scale = lax.rsqrt(square * (1.0 / full) + 1e-06)
        gate_act = sum(dot(p, w) for p, w in zip(pieces, gate_w)) * row_scale
        up_act = sum(dot(p, w) for p, w in zip(pieces, up_w)) * row_scale
        hidden = (jax.nn.silu(gate_act) * up_act).astype(BF)
        results.append([dot(hidden, w).astype(BF) for w in down_w])
    (a0, a1, a2, a3), (b0, b1, b2, b3) = results

    add = lambda p, q: (p.astype(F32) + q.astype(F32)).astype(BF)
    via_a = shift(a2, "section", 1)
    via_b = shift(b2, "section", -1)
    near_b = shift(b1, "section", 1)
    near_a = shift(a3, "section", -1)
    back_a = shift(add(a1, via_a), "section", 1)
    back_b = shift(add(b3, via_b), "section", -1)
    total_a = (a0.astype(F32) + near_a.astype(F32) + back_a.astype(F32)).astype(BF)
    total_b = (b0.astype(F32) + near_b.astype(F32) + back_b.astype(F32)).astype(BF)
    total = jnp.concatenate([total_a, total_b], axis=0).reshape(expert_total, capacity, columns)
    returned = lax.all_to_all(total, ("dp", "expert"), split_axis=0, concat_axis=0, tiled=True)
    returned = returned.reshape(rows, columns)
    expert_sum = dot(gate_high, returned) + dot(gate_low, returned)
    return (proj_own.astype(F32) + expert_sum).astype(BF)


def solution(mesh):
    return jax.shard_map(
        per_device,
        mesh=mesh,
        in_specs=(
            P(("dp", "expert"), None),
            P(("dp", "expert"), None),
            P(None, "section"),
            P("section", None),
            P("dp", "section"),
            P(("dp", "expert"), None),
            P(("dp", "expert"), None),
            P(("dp", "expert"), None, "section"),
            P(("dp", "expert"), None, "section"),
            P(("dp", "expert"), "section", None),
        ),
        out_specs=P(("dp", "expert"), "section"),
        check_vma=False,
    )
```

```python
import functools
import math

import jax
import jax.numpy as jnp
from jax import lax
from jax.experimental import pallas as pl
from jax.experimental.pallas import tpu as pltpu
from jax.sharding import PartitionSpec as P


D_VIT = 1152
HEADS = 16
TOP = 6
BF = jnp.bfloat16
F32 = jnp.float32

LATE = 128
VMEM = pl.BlockSpec(memory_space=pltpu.VMEM)
SMEM = pl.BlockSpec(memory_space=pltpu.SMEM)


def params(mib):
    return pltpu.CompilerParams(vmem_limit_bytes=mib * 2**20)


def dot(a, b):
    return jnp.dot(a, b, preferred_element_type=F32)


def dot_tn(a, b):
    return lax.dot_general(a, b, (((0,), (0,)), ((), ())), preferred_element_type=F32)


def dot_nt(a, b):
    return lax.dot_general(a, b, (((1,), (1,)), ((), ())), preferred_element_type=F32)


def shift(value, axis, step):
    count = lax.axis_size(axis)
    return lax.ppermute(value, axis, [(i, (i + step) % count) for i in range(count)])


def partner(value):
    count = lax.axis_size("dp")
    return lax.ppermute(value, "dp", [(i, i ^ 1) for i in range(count)])


def layer_norm(values):
    center = values - jnp.mean(values, axis=-1, keepdims=True)
    spread = jnp.mean(center * center, axis=-1, keepdims=True)
    return center * lax.rsqrt(spread + 1e-06)


def route_tables(routes, gates, expert_total, capacity):
    rows = routes.shape[0]
    ids = jnp.arange(expert_total, dtype=jnp.int32)
    named = routes[:, :, None] == ids[None, None, :]
    member = jnp.any(named, axis=1)
    weight = jnp.sum(jnp.where(named, gates[:, :, None], 0.0), axis=1)
    places = jnp.arange(rows, dtype=jnp.int32)
    before = (places[:, None] > places[None, :]).astype(BF)
    slot = dot(before, member.astype(BF))
    slot = jnp.where(member, slot, 255.0).astype(BF)
    lanes = jnp.arange(expert_total * capacity, dtype=jnp.int32)
    spread = (lanes[None, :] // capacity == ids[:, None]).astype(BF)
    hit = dot(slot, spread) == (lanes % capacity).astype(F32)[None, :]
    pick = dot_tn(spread, slot.T) == (lanes % capacity).astype(F32)[:, None]
    high = weight.astype(BF)
    low = (weight - high.astype(F32)).astype(BF)
    gate_high = jnp.where(hit, dot(high, spread), 0.0).astype(BF)
    gate_low = jnp.where(hit, dot(low, spread), 0.0).astype(BF)
    return pick.astype(BF), jnp.concatenate([gate_high, gate_low], axis=0)


def project_body(place, patches, *refs):
    att, out_rows, rows, pick = refs[0:4], refs[4:8], refs[8:16], refs[16]
    own_out, late_out, slot_out = refs[17:20]
    att_v, out_v, proj_v, enc, sems = refs[20:]
    row_y, core = place[0], place[1]
    half = rows[0].shape[0]
    copies = []
    for d in range(4):
        copies.append(pltpu.make_async_copy(att[d], att_v.at[d], sems.at[d]))
        copies.append(pltpu.make_async_copy(out_rows[d], out_v.at[d], sems.at[4 + d]))
    for d in range(4):
        mine = pl.multiple_of(core * half, 64)
        other = pl.multiple_of((1 - core) * half, 64)
        copies.append(pltpu.make_async_copy(rows[d], proj_v.at[d, pl.ds(mine, half)], sems.at[8 + d]))
        copies.append(pltpu.make_async_copy(rows[4 + d], proj_v.at[d, pl.ds(other, half)], sems.at[12 + d]))
    for c in copies:
        c.start()
    for c in copies[:8]:
        c.wait()
    step = 128
    for r in range(patches.shape[0] // step):
        at = pl.ds(r * step, step)
        total = patches[at, :].astype(F32)
        for d in range(4):
            total += dot_tn(att_v[d, :, at], out_v[d])
        for q in range(enc.shape[0]):
            enc[q, at, :] = total[:, q * 128 : (q + 1) * 128]
    for c in copies[8:]:
        c.wait()
    merged = patches.shape[0] // 4
    acc = jnp.zeros(own_out.shape, F32)
    for d in range(4):
        j = lax.rem(row_y + 4 - d, 4)
        block = [enc[q, pl.ds(j, merged, stride=4), :].astype(BF) for q in range(enc.shape[0])]
        acc += dot(jnp.concatenate(block, axis=1), proj_v[d])
    own = acc.astype(BF)
    own_out[...] = own
    early = slot_out.shape[1]
    late_out[...] = own[:, early:]
    slot_out[...] = dot(pick[...], own[:, :early]).astype(BF)


def project(place, patches, att, out_rows, proj_rows, pick):
    merged = patches.shape[0] // 4
    columns = proj_rows[0].shape[1]
    half = proj_rows[0].shape[0]
    slots = pick.shape[0]
    anyspace = pl.BlockSpec(memory_space=pl.ANY)
    return pl.pallas_call(
        project_body,
        out_shape=(
            jax.ShapeDtypeStruct((merged, columns), BF),
            jax.ShapeDtypeStruct((merged, LATE), BF),
            jax.ShapeDtypeStruct((slots, columns - LATE), BF),
        ),
        in_specs=[SMEM, VMEM] + [anyspace] * 16 + [VMEM],
        out_specs=(VMEM, VMEM, VMEM),
        scratch_shapes=[
            pltpu.VMEM((4,) + att[0].shape, BF),
            pltpu.VMEM((4,) + out_rows[0].shape, BF),
            pltpu.VMEM((4, 2 * half, columns), BF),
            pltpu.VMEM((patches.shape[1] // 128, patches.shape[0], 128), F32),
            pltpu.SemaphoreType.DMA((16,)),
        ],
        compiler_params=params(24),
        name="project",
    )(place, patches, *att, *out_rows, *proj_rows, pick)


def pick_body(pick, late, out):
    out[...] = dot(pick[...], late[...]).astype(BF)


def pick_rows(pick, late):
    return pl.pallas_call(
        pick_body,
        out_shape=jax.ShapeDtypeStruct((pick.shape[0], late.shape[1]), BF),
        compiler_params=params(8),
        name="pick_rows",
    )(pick, late)


def squares(x):
    wide = x.astype(F32)
    wide = wide * wide
    return sum(wide[:, q * 128 : (q + 1) * 128] for q in range(x.shape[1] // 128))


def lanes_of(section, offset, sections, columns, width):
    return pl.ds(pl.multiple_of(lax.rem(section + offset, sections) * columns, 128), width)


ROWS = 256


def hbm(shape, dtype):
    return pltpu.MemorySpace.HBM(shape, dtype)


def keep(*values):
    return [pltpu.with_memory_space_constraint(v, pltpu.MemorySpace.HBM) for v in values]


def rows_spec(width, index=lambda r: (r, 0)):
    return pl.BlockSpec((ROWS, width), index)


def fixed_spec(value):
    return pl.BlockSpec(value.shape, lambda r: (0, 0), pipeline_mode=pl.Buffered(1))


def up_body(columns, sections, place, own, left, right, w, acc_out, square_out):
    width = own.shape[1]
    acc = jnp.zeros((ROWS, w.shape[0]), F32)
    square = jnp.zeros((ROWS, 128), F32)
    for o, piece in ((0, own), (3, left), (1, right)):
        x = piece[...]
        acc += dot_nt(x, w[:, lanes_of(place[0], o, sections, columns, width)])
        square += squares(x)
    acc_out[...] = acc
    square_out[...] = square


def up(columns, sections, place, own, left, right, w):
    rows, width = own.shape
    return pl.pallas_call(
        functools.partial(up_body, columns, sections),
        out_shape=(hbm((rows, w.shape[0]), F32), hbm((rows, 128), F32)),
        grid=(rows // ROWS,),
        in_specs=[SMEM] + [rows_spec(width)] * 3 + [fixed_spec(w)],
        out_specs=(rows_spec(w.shape[0]), rows_spec(128)),
        compiler_params=params(20),
        name="up",
    )(place, *keep(own, left, right, w))


def hidden_body(columns, sections, place, acc, square, late, far_a, far_b, w, w_late, w_down, hid_out, to_a, to_b):
    hidden_count = w_down.shape[0]
    width = far_a.shape[1]
    r, blocks = pl.program_id(0), pl.num_programs(0)
    in_a = r < blocks // 2
    x = jnp.where(in_a, far_a[...], far_b[...])
    y = late[...]
    two_away = lanes_of(place[0], 2, sections, columns, width)
    total = acc[...] + dot_nt(x, w[:, two_away])
    total += dot_nt(y, w_late[...])
    square_sum = square[...] + squares(x) + squares(y)
    mean = jnp.sum(square_sum, axis=-1, keepdims=True) * (1.0 / (columns * sections))
    row_scale = lax.rsqrt(mean + 1e-06)
    gate = total[:, :hidden_count] * row_scale
    upper = total[:, hidden_count:] * row_scale
    hidden = (gate / (1.0 + jnp.exp(-gate)) * upper).astype(BF)
    hid_out[...] = hidden
    part = dot(hidden, w_down[:, two_away]).astype(BF)

    @pl.when(in_a)
    def _():
        to_a[...] = part

    @pl.when(jnp.logical_not(in_a))
    def _():
        to_b[...] = part


def hidden_units(columns, sections, place, acc, square, late, far_a, far_b, w, w_late, w_down):
    rows, width = acc.shape[0], far_a.shape[1]
    half = rows // 2 // ROWS
    spec_a = rows_spec(width, lambda r: (jnp.minimum(r, half - 1), 0))
    spec_b = rows_spec(width, lambda r: (jnp.maximum(r - half, 0), 0))
    return pl.pallas_call(
        functools.partial(hidden_body, columns, sections),
        out_shape=(hbm((rows, w_down.shape[0]), BF), hbm((rows // 2, width), BF), hbm((rows // 2, width), BF)),
        grid=(rows // ROWS,),
        in_specs=[SMEM, rows_spec(acc.shape[1]), rows_spec(128), rows_spec(late.shape[1]), spec_a, spec_b]
        + [fixed_spec(w), fixed_spec(w_late), fixed_spec(w_down)],
        out_specs=(rows_spec(w_down.shape[0]), spec_a, spec_b),
        compiler_params=params(24),
        name="hidden_units",
    )(place, *keep(acc, square, late, far_a, far_b, w, w_late, w_down))


def down_body(columns, sections, place, hidden, w_down, w_late, right_out, left_out, here_out, late_out):
    width = here_out.shape[1]
    h = hidden[...]
    for o, out in ((1, right_out), (3, left_out), (0, here_out)):
        out[...] = dot(h, w_down[:, lanes_of(place[0], o, sections, columns, width)]).astype(BF)
    late_out[...] = dot(h, w_late[...]).astype(BF)


def down(columns, sections, place, hidden, w_down, w_late):
    rows = hidden.shape[0]
    widths = [columns - LATE] * 3 + [LATE * sections]
    return pl.pallas_call(
        functools.partial(down_body, columns, sections),
        out_shape=[hbm((rows, n), BF) for n in widths],
        grid=(rows // ROWS,),
        in_specs=[SMEM, rows_spec(hidden.shape[1]), fixed_spec(w_down), fixed_spec(w_late)],
        out_specs=[rows_spec(n) for n in widths],
        compiler_params=params(16),
        name="down",
    )(place, *keep(hidden, w_down, w_late))


def weigh_body(gates, late, out):
    both = dot(gates[...], late[...])
    merged = both.shape[0] // 2
    total = (both[:merged] + both[merged:]).astype(BF)
    for s in range(out.shape[0]):
        out[s] = total[:, s * LATE : (s + 1) * LATE]


def weigh(gates, late, sections):
    return pl.pallas_call(
        weigh_body,
        out_shape=jax.ShapeDtypeStruct((sections, gates.shape[0] // 2, LATE), BF),
        compiler_params=params(12),
        name="weigh",
    )(gates, late)


def combine_body(gates, own, late, early, out):
    merged, _ = own.shape
    width = early.shape[1]
    both = dot(gates[...], early[...])
    out[:, :width] = (own[:, :width].astype(F32) + both[:merged] + both[merged:]).astype(BF)
    total = own[:, width:].astype(F32)
    for s in range(late.shape[0]):
        total += late[s].astype(F32)
    out[:, width:] = total.astype(BF)


def combine(gates, own, late, early):
    return pl.pallas_call(
        combine_body,
        out_shape=jax.ShapeDtypeStruct(own.shape, BF),
        compiler_params=params(12),
        name="combine",
    )(gates, own, late, early)


def per_device(patches, lengths, w_qkv, w_out, w_proj, routes, gates, w_gate, w_up, w_down):
    data_count = lax.axis_size("dp")
    owner_count = lax.axis_size("expert")
    sections = lax.axis_size("section")
    patch_rows, _ = patches.shape
    merged_count = patch_rows // 4
    head_dim = D_VIT // HEADS
    local_heads = w_qkv.shape[1] // (3 * head_dim)
    scale = 1.0 / math.sqrt(head_dim)
    expert_total = data_count * owner_count
    capacity = max(2, min(merged_count, 2 * merged_count * TOP // expert_total))
    columns = w_proj.shape[1]
    early = columns - LATE
    place = jnp.stack([lax.axis_index("section")]).astype(jnp.int32)
    dp_place = jnp.stack([lax.axis_index("dp") // 2, lax.axis_index("dp") % 2]).astype(jnp.int32)

    out_rows, mine = [w_out], [w_proj]
    for d in (1, 2, 3):
        mine.append(shift(w_proj, "dp", 2 * d))
        out_rows.append(shift(w_out, "section", d))
    proj_rows = mine + [partner(m) for m in mine]

    normed_in = layer_norm(patches.astype(F32)).astype(BF)
    packed = dot(normed_in, w_qkv).astype(BF)
    packed = packed.reshape(patch_rows, local_heads, 3, head_dim)
    query = packed[:, :, 0]
    key_part = packed[:, :, 1]
    value_part = packed[:, :, 2]
    ends = jnp.cumsum(lengths[0]) * 4
    places = jnp.arange(patch_rows, dtype=jnp.int32)
    segment = jnp.sum((places[:, None] >= ends[None, :]).astype(jnp.int32), axis=1)
    same = segment[:, None] == segment[None, :]
    scores = jnp.einsum("qhd,khd->hqk", query, key_part, preferred_element_type=F32) * scale
    scores = jnp.where(same[None], scores, -jnp.inf)
    peak = jnp.max(scores, axis=-1, keepdims=True)
    weights = jnp.where(same[None], jnp.exp(scores - peak), 0.0)
    probs = (weights / jnp.sum(weights, axis=-1, keepdims=True)).astype(BF)
    attended = jnp.einsum("hqk,khd->hdq", probs, value_part, preferred_element_type=F32)
    attended = attended.astype(BF).reshape(local_heads * head_dim, patch_rows)

    att = [attended]
    for d in (1, 2, 3):
        att.append(shift(attended, "section", d))
    pick, gate_rows = route_tables(routes, gates, expert_total, capacity)
    w_both = jnp.concatenate([w_gate[0].T, w_up[0].T], axis=0)
    last = lambda w: jnp.concatenate([w[:, s * columns + early : (s + 1) * columns] for s in range(sections)], axis=1)
    w_late, down_late = last(w_both), last(w_down[0])
    proj_own, late, outgoing = project(dp_place, patches, att, out_rows, proj_rows, pick)

    rows = expert_total * capacity

    def exchange(value):
        wide = value.reshape(expert_total, capacity, value.shape[1])
        wide = lax.all_to_all(wide, ("dp", "expert"), split_axis=0, concat_axis=0, tiled=True)
        return wide.reshape(value.shape)

    own = exchange(outgoing)
    late_all = lax.all_gather(late, "section", axis=1, tiled=True)
    late_rows = pick_rows(pick, late_all)
    late_rows = exchange(late_rows)
    left = shift(own, "section", 1)
    right = shift(own, "section", -1)
    far_a = shift(left[: rows // 2], "section", 1)
    far_b = shift(right[rows // 2 :], "section", -1)
    acc, square = up(columns, sections, place, own, left, right, w_both)
    hidden, to_a, to_b = hidden_units(
        columns, sections, place, acc, square, late_rows, far_a, far_b, w_both, w_late, w_down[0]
    )
    via_a = shift(to_a, "section", 1)
    via_b = shift(to_b, "section", -1)
    to_right, to_left, here, late_out = down(columns, sections, place, hidden, w_down[0], down_late)
    late_back = exchange(late_out)
    top, bottom = to_right[: rows // 2], to_right[rows // 2 :]
    to_right = jnp.concatenate([(top.astype(F32) + via_a.astype(F32)).astype(BF), bottom], axis=0)
    top, bottom = to_left[: rows // 2], to_left[rows // 2 :]
    to_left = jnp.concatenate([top, (bottom.astype(F32) + via_b.astype(F32)).astype(BF)], axis=0)
    from_left = shift(to_right, "section", 1)
    from_right = shift(to_left, "section", -1)
    total = (here.astype(F32) + from_left.astype(F32) + from_right.astype(F32)).astype(BF)
    returned = exchange(total)
    late_sum = weigh(gate_rows, late_back, sections)
    late_sum = lax.all_to_all(late_sum, "section", split_axis=0, concat_axis=0, tiled=True)
    return combine(gate_rows, proj_own, late_sum, returned)


def solution(mesh):
    return jax.shard_map(
        per_device,
        mesh=mesh,
        in_specs=(
            P(("dp", "expert"), None),
            P(("dp", "expert"), None),
            P(None, "section"),
            P("section", None),
            P("dp", "section"),
            P(("dp", "expert"), None),
            P(("dp", "expert"), None),
            P(("dp", "expert"), None, "section"),
            P(("dp", "expert"), None, "section"),
            P(("dp", "expert"), "section", None),
        ),
        out_specs=P(("dp", "expert"), "section"),
        check_vma=False,
    )
```

```python
import functools
import math

import jax
import jax.numpy as jnp
from jax import lax
from jax.experimental import pallas as pl
from jax.experimental.pallas import tpu as pltpu
from jax.sharding import PartitionSpec as P


D_VIT = 1152
HEADS = 16
TOP = 6
BF = jnp.bfloat16
F32 = jnp.float32

LATE = 128
VMEM = pl.BlockSpec(memory_space=pltpu.VMEM)
SMEM = pl.BlockSpec(memory_space=pltpu.SMEM)


def params(mib):
    return pltpu.CompilerParams(vmem_limit_bytes=mib * 2**20)


def dot(a, b):
    return jnp.dot(a, b, preferred_element_type=F32)


def dot_tn(a, b):
    return lax.dot_general(a, b, (((0,), (0,)), ((), ())), preferred_element_type=F32)


def dot_nt(a, b):
    return lax.dot_general(a, b, (((1,), (1,)), ((), ())), preferred_element_type=F32)


def shift(value, axis, step):
    count = lax.axis_size(axis)
    return lax.ppermute(value, axis, [(i, (i + step) % count) for i in range(count)])


def partner(value):
    count = lax.axis_size("dp")
    return lax.ppermute(value, "dp", [(i, i ^ 1) for i in range(count)])


def route_tables(routes, gates, expert_total, capacity):
    rows = routes.shape[0]
    ids = jnp.arange(expert_total, dtype=jnp.int32)
    named = routes[:, :, None] == ids[None, None, :]
    member = jnp.any(named, axis=1)
    weight = jnp.sum(jnp.where(named, gates[:, :, None], 0.0), axis=1)
    places = jnp.arange(rows, dtype=jnp.int32)
    before = (places[:, None] > places[None, :]).astype(BF)
    slot = dot(before, member.astype(BF))
    slot = jnp.where(member, slot, 255.0).astype(BF)
    lanes = jnp.arange(expert_total * capacity, dtype=jnp.int32)
    spread = (lanes[None, :] // capacity == ids[:, None]).astype(BF)
    hit = dot(slot, spread) == (lanes % capacity).astype(F32)[None, :]
    pick = dot_tn(spread, slot.T) == (lanes % capacity).astype(F32)[:, None]
    high = weight.astype(BF)
    low = (weight - high.astype(F32)).astype(BF)
    gate_high = jnp.where(hit, dot(high, spread), 0.0).astype(BF)
    gate_low = jnp.where(hit, dot(low, spread), 0.0).astype(BF)
    return pick.astype(BF), jnp.concatenate([gate_high, gate_low], axis=0)


def hbm(shape, dtype):
    return pltpu.MemorySpace.HBM(shape, dtype)


def keep(*values):
    return [pltpu.with_memory_space_constraint(v, pltpu.MemorySpace.HBM) for v in values]


def attend_body(head_dim, ends, patches, w, out, qkv, bias, heads):
    rows = patches.shape[0]
    values = patches[...].astype(F32)
    center = values - jnp.mean(values, axis=-1, keepdims=True)
    spread = jnp.mean(center * center, axis=-1, keepdims=True)
    normed = (center * lax.rsqrt(spread + 1e-06)).astype(BF)
    qkv[...] = dot_nt(w[...], normed)
    images = ends.shape[0]

    def image_of(axis):
        place = lax.broadcasted_iota(jnp.int32, (rows, 1) if axis == 0 else (1, rows), axis)
        return sum((place >= ends[i]).astype(jnp.int32) for i in range(images))

    bias[...] = jnp.where(image_of(0) == image_of(1), 0.0, -1e30)

    def one(h, carry):
        base = pl.multiple_of(h * 3 * head_dim, 8)
        query = (qkv[pl.ds(base, head_dim), :] * (1.0 / math.sqrt(head_dim))).astype(BF)
        key = qkv[pl.ds(base + head_dim, head_dim), :].astype(BF)
        value = qkv[pl.ds(base + 2 * head_dim, head_dim), :].astype(BF)
        scores = dot_tn(key, query) + bias[...]
        weights = jnp.exp(scores - jnp.max(scores, axis=0, keepdims=True))
        total = jnp.sum(weights, axis=0, keepdims=True)
        heads[pl.ds(pl.multiple_of(h * head_dim, 8), head_dim), :] = dot(value, weights.astype(BF)) / total
        return carry

    lax.fori_loop(0, w.shape[0] // (3 * head_dim), one, 0)
    out[...] = heads[...].astype(BF)


def attend(head_dim, ends, patches, w):
    rows = patches.shape[0]
    features = w.shape[0]
    return pl.pallas_call(
        functools.partial(attend_body, head_dim),
        out_shape=hbm((features // 3, rows), BF),
        in_specs=[SMEM, VMEM, VMEM],
        out_specs=VMEM,
        scratch_shapes=[
            pltpu.VMEM((features, rows), F32),
            pltpu.VMEM((rows, rows), F32),
            pltpu.VMEM((features // 3, rows), F32),
        ],
        compiler_params=params(24),
        name="attend",
    )(ends, patches, w)


def project_body(place, patches, *refs):
    att, w_out, out_rows, out_other, rows, pick = refs[0:4], refs[4], refs[5:8], refs[8], refs[9:17], refs[17]
    own_out, late_out, slot_out = refs[18:21]
    att_v, out_v, proj_v, enc, sems = refs[21:]
    row_y, core = place[0], place[1]
    half = rows[0].shape[0]
    copies = []
    for d in range(4):
        copies.append(pltpu.make_async_copy(att[d], att_v.at[d], sems.at[d]))
    copies.append(pltpu.make_async_copy(w_out, out_v.at[0], sems.at[4]))
    part = out_rows[0].shape[0]
    for d in (1, 2, 3):
        mine = pl.multiple_of(core * part, 16)
        other = pl.multiple_of((1 - core) * part, 16)
        copies.append(pltpu.make_async_copy(out_rows[d - 1], out_v.at[d, pl.ds(mine, part)], sems.at[4 + d]))
        copies.append(
            pltpu.make_async_copy(out_other.at[pl.ds((d - 1) * part, part)], out_v.at[d, pl.ds(other, part)], sems.at[15 + d])
        )
    first = len(copies)
    for d in range(4):
        mine = pl.multiple_of(core * half, 64)
        other = pl.multiple_of((1 - core) * half, 64)
        copies.append(pltpu.make_async_copy(rows[d], proj_v.at[d, pl.ds(mine, half)], sems.at[8 + d]))
        copies.append(pltpu.make_async_copy(rows[4 + d], proj_v.at[d, pl.ds(other, half)], sems.at[12 + d]))
    for c in copies:
        c.start()
    for c in copies[:first]:
        c.wait()
    step = 128
    for r in range(patches.shape[0] // step):
        at = pl.ds(r * step, step)
        total = patches[at, :].astype(F32)
        for d in range(4):
            total += dot_tn(att_v[d, :, at], out_v[d])
        for q in range(enc.shape[0]):
            enc[q, at, :] = total[:, q * 128 : (q + 1) * 128]
    for c in copies[first:]:
        c.wait()
    merged = patches.shape[0] // 4
    acc = jnp.zeros(own_out.shape, F32)
    for d in range(4):
        j = lax.rem(row_y + 4 - d, 4)
        block = [enc[q, pl.ds(j, merged, stride=4), :].astype(BF) for q in range(enc.shape[0])]
        acc += dot(jnp.concatenate(block, axis=1), proj_v[d])
    own = acc.astype(BF)
    own_out[...] = own
    early = slot_out.shape[1]
    late_out[...] = own[:, early:]
    slot_out[...] = dot(pick[...], own[:, :early]).astype(BF)


def project(place, patches, att, w_out, out_rows, out_other, proj_rows, pick):
    merged = patches.shape[0] // 4
    columns = proj_rows[0].shape[1]
    half = proj_rows[0].shape[0]
    slots = pick.shape[0]
    anyspace = pl.BlockSpec(memory_space=pl.ANY)
    return pl.pallas_call(
        project_body,
        out_shape=(
            hbm((merged, columns), BF),
            jax.ShapeDtypeStruct((merged, LATE), BF),
            hbm((slots, columns - LATE), BF),
        ),
        in_specs=[SMEM, VMEM] + [anyspace] * 17 + [VMEM],
        out_specs=(VMEM, VMEM, VMEM),
        scratch_shapes=[
            pltpu.VMEM((4,) + att[0].shape, BF),
            pltpu.VMEM((4,) + w_out.shape, BF),
            pltpu.VMEM((4, 2 * half, columns), BF),
            pltpu.VMEM((patches.shape[1] // 128, patches.shape[0], 128), F32),
            pltpu.SemaphoreType.DMA((19,)),
        ],
        compiler_params=params(24),
        name="project",
    )(place, patches, *att, w_out, *out_rows, out_other, *proj_rows, pick)


def pick_body(pick, late, out):
    out[...] = dot(pick[...], late[...]).astype(BF)


def pick_rows(pick, late):
    return pl.pallas_call(
        pick_body,
        out_shape=hbm((pick.shape[0], late.shape[1]), BF),
        compiler_params=params(8),
        name="pick_rows",
    )(pick, late)


def squares(x):
    wide = x.astype(F32)
    wide = wide * wide
    return sum(wide[:, q * 128 : (q + 1) * 128] for q in range(x.shape[1] // 128))


ROWS = 384


def rows_spec(width, index=lambda r, *place: (r, 0)):
    return pl.BlockSpec((ROWS, width), index)


def lane_block(height, width, offset, sections):
    return pl.BlockSpec(
        (height, width), lambda r, place: (0, lax.rem(place[0] + offset, sections)), pipeline_mode=pl.Buffered(1)
    )


def whole_block(shape):
    return pl.BlockSpec(shape, lambda r, place: (0, 0), pipeline_mode=pl.Buffered(1))


def over_rows(body, rows, in_specs, out_specs, out_shape, operands):
    return pl.pallas_call(
        body,
        grid_spec=pltpu.PrefetchScalarGridSpec(
            num_scalar_prefetch=1, grid=(rows // ROWS,), in_specs=in_specs, out_specs=out_specs
        ),
        out_shape=out_shape,
        compiler_params=params(20),
    )(*operands)


def up_body(place, own, left, right, w_own, w_left, w_right, acc_out, square_out):
    width = own.shape[1]
    acc = jnp.zeros(acc_out.shape, F32)
    square = jnp.zeros(square_out.shape, F32)
    for piece, w in ((own, w_own), (left, w_left), (right, w_right)):
        x = piece[...]
        acc += dot_nt(x, w[:, :width])
        square += squares(x)
    acc_out[...] = acc
    square_out[...] = square


def up(columns, sections, place, own, left, right, w):
    rows, width = own.shape
    count = w.shape[0]
    return over_rows(
        up_body,
        rows,
        [rows_spec(width)] * 3 + [lane_block(count, columns, o, sections) for o in (0, 3, 1)],
        (rows_spec(count), rows_spec(128)),
        (hbm((rows, count), F32), hbm((rows, 128), F32)),
        (place, *keep(own, left, right, w, w, w)),
    )


def hidden_body(full, place, acc, square, late, far_a, far_b, w, w_late, w_down, hid_out, to_a, to_b):
    hidden_count = w_down.shape[0]
    width = far_a.shape[1]
    in_a = pl.program_id(0) < pl.num_programs(0) // 2
    x = jnp.where(in_a, far_a[...], far_b[...])
    y = late[...]
    total = acc[...] + dot_nt(x, w[:, :width])
    total += dot_nt(y, w_late[...])
    square_sum = square[...] + squares(x) + squares(y)
    mean = jnp.sum(square_sum, axis=-1, keepdims=True) * (1.0 / full)
    row_scale = lax.rsqrt(mean + 1e-06)
    gate = total[:, :hidden_count] * row_scale
    upper = total[:, hidden_count:] * row_scale
    hidden = (gate / (1.0 + jnp.exp(-gate)) * upper).astype(BF)
    hid_out[...] = hidden
    part = dot(hidden, w_down[:, :width]).astype(BF)

    @pl.when(in_a)
    def _():
        to_a[...] = part

    @pl.when(jnp.logical_not(in_a))
    def _():
        to_b[...] = part


def hidden_units(columns, sections, place, acc, square, late, far_a, far_b, w, w_late, w_down):
    rows, width = acc.shape[0], far_a.shape[1]
    half = rows // 2 // ROWS
    spec_a = rows_spec(width, lambda r, place: (jnp.minimum(r, half - 1), 0))
    spec_b = rows_spec(width, lambda r, place: (jnp.maximum(r - half, 0), 0))
    return over_rows(
        functools.partial(hidden_body, columns * sections),
        rows,
        [rows_spec(acc.shape[1]), rows_spec(128), rows_spec(late.shape[1]), spec_a, spec_b]
        + [lane_block(w.shape[0], columns, 2, sections), whole_block(w_late.shape)]
        + [lane_block(w_down.shape[0], columns, 2, sections)],
        (rows_spec(w_down.shape[0]), spec_a, spec_b),
        (hbm((rows, w_down.shape[0]), BF), hbm((rows // 2, width), BF), hbm((rows // 2, width), BF)),
        (place, *keep(acc, square, late, far_a, far_b, w, w_late, w_down)),
    )


def down_body(count, place, hidden, *refs):
    h = hidden[...]
    for w, out in zip(refs[:count], refs[count:]):
        out[...] = dot(h, w[:, : out.shape[1]]).astype(BF)


def down(columns, sections, offsets, place, hidden, w, width):
    rows, height = hidden.shape
    count = len(offsets) or 1
    blocks = [lane_block(height, columns, o, sections) for o in offsets] or [whole_block(w.shape)]
    return over_rows(
        functools.partial(down_body, count),
        rows,
        [rows_spec(height)] + blocks,
        [rows_spec(width)] * count,
        [hbm((rows, width), BF)] * count,
        (place, *keep(hidden, *[w] * count)),
    )


def cut_body(left, right, top, bottom):
    top[...] = left[...]
    bottom[...] = right[...]


def cut(left, right):
    rows, width = left.shape
    half = rows // 2 // ROWS
    return pl.pallas_call(
        cut_body,
        out_shape=(hbm((rows // 2, width), BF),) * 2,
        grid=(half,),
        in_specs=[rows_spec(width), rows_spec(width, lambda r: (r + half, 0))],
        out_specs=[rows_spec(width)] * 2,
        compiler_params=params(8),
        name="cut",
    )(*keep(left, right))


def add_body(right, left, via_a, via_b, right_out, left_out):
    right_out[...] = (right[...].astype(F32) + via_a[...].astype(F32)).astype(BF)
    left_out[...] = (left[...].astype(F32) + via_b[...].astype(F32)).astype(BF)


def add(right, left, via_a, via_b):
    rows, width = right.shape
    half = rows // 2 // ROWS
    whole = [rows_spec(width), rows_spec(width, lambda r: (r + half, 0))]
    return pl.pallas_call(
        add_body,
        out_shape=(hbm(right.shape, BF), hbm(left.shape, BF)),
        grid=(half,),
        in_specs=whole + [rows_spec(width)] * 2,
        out_specs=whole,
        input_output_aliases={0: 0, 1: 1},
        compiler_params=params(8),
        name="add",
    )(*keep(right, left, via_a, via_b))


def weigh_body(gates, late, out):
    both = dot(gates[...], late[...])
    merged = both.shape[0] // 2
    out[...] = (both[:merged] + both[merged:]).astype(BF)


def weigh(gates, late):
    return pl.pallas_call(
        weigh_body,
        out_shape=jax.ShapeDtypeStruct((gates.shape[0] // 2, late.shape[1]), BF),
        compiler_params=params(12),
        name="weigh",
    )(gates, late)


def combine_body(sections, place, gates, own, late, early, out):
    merged, _ = own.shape
    width = early.shape[1]
    both = dot(gates[...], early[...])
    out[:, :width] = (own[:, :width].astype(F32) + both[:merged] + both[merged:]).astype(BF)
    total = own[:, width:].astype(F32)
    for s in range(sections):
        first = s * sections * LATE + place[0] * LATE
        total += late[:, pl.ds(pl.multiple_of(first, LATE), LATE)].astype(F32)
    out[:, width:] = total.astype(BF)


def combine(sections, place, gates, own, late, early):
    return pl.pallas_call(
        functools.partial(combine_body, sections),
        out_shape=jax.ShapeDtypeStruct(own.shape, BF),
        in_specs=[SMEM] + [VMEM] * 4,
        out_specs=VMEM,
        compiler_params=params(12),
        name="combine",
    )(place, *keep(gates, own, late), early)


def per_device(patches, lengths, w_qkv, w_out, w_proj, routes, gates, w_gate, w_up, w_down):
    data_count = lax.axis_size("dp")
    owner_count = lax.axis_size("expert")
    sections = lax.axis_size("section")
    merged_count = patches.shape[0] // 4
    expert_total = data_count * owner_count
    capacity = max(2, min(merged_count, 2 * merged_count * TOP // expert_total))
    columns = w_proj.shape[1]
    early = columns - LATE
    place = jnp.stack([lax.axis_index("section")]).astype(jnp.int32)
    dp_place = jnp.stack([lax.axis_index("dp") // 2, lax.axis_index("dp") % 2]).astype(jnp.int32)

    out_rows, mine = [], [w_proj]
    out_half = lax.dynamic_slice_in_dim(w_out, dp_place[1] * (w_out.shape[0] // 2), w_out.shape[0] // 2, axis=0)
    for d in (1, 2, 3):
        mine.append(shift(w_proj, "dp", 2 * d))
        out_rows.append(shift(out_half, "section", d))
    proj_rows = mine + [partner(m) for m in mine]
    out_other = partner(jnp.concatenate(out_rows, axis=0))

    ends = jnp.cumsum(lengths[0]).astype(jnp.int32) * 4
    attended = attend(D_VIT // HEADS, ends, patches, w_qkv.T)

    att = [attended]
    for d in (1, 2, 3):
        att.append(shift(attended, "section", d))
    pick, gate_rows = route_tables(routes, gates, expert_total, capacity)
    w_both = jnp.concatenate([w_gate[0].T, w_up[0].T], axis=0)
    last = lambda w: jnp.concatenate([w[:, s * columns + early : (s + 1) * columns] for s in range(sections)], axis=1)
    w_late, down_late = last(w_both), last(w_down[0])
    proj_own, late, outgoing = project(dp_place, patches, att, w_out, out_rows, out_other, proj_rows, pick)

    def exchange(value):
        wide = value.reshape(expert_total, capacity, value.shape[1])
        wide = lax.all_to_all(wide, ("dp", "expert"), split_axis=0, concat_axis=0, tiled=True)
        return wide.reshape(value.shape)

    own = exchange(outgoing)
    late_all = lax.all_gather(late, "section", axis=1, tiled=True)
    late_rows = pick_rows(pick, late_all)
    late_rows = exchange(late_rows)
    left = shift(own, "section", 1)
    right = shift(own, "section", -1)
    top, bottom = cut(left, right)
    far_a = shift(top, "section", 1)
    far_b = shift(bottom, "section", -1)
    acc, square = up(columns, sections, place, own, left, right, w_both)
    hidden, to_a, to_b = hidden_units(
        columns, sections, place, acc, square, late_rows, far_a, far_b, w_both, w_late, w_down[0]
    )
    via_a = shift(to_a, "section", 1)
    via_b = shift(to_b, "section", -1)
    (late_out,) = down(columns, sections, (), place, hidden, down_late, LATE * sections)
    late_back = exchange(late_out)
    to_right, to_left, here = down(columns, sections, (1, 3, 0), place, hidden, w_down[0], early)
    to_right, to_left = add(to_right, to_left, via_a, via_b)
    from_left = shift(to_right, "section", 1)
    from_right = shift(to_left, "section", -1)
    total = (here.astype(F32) + from_left.astype(F32) + from_right.astype(F32)).astype(BF)
    returned = exchange(total)
    late_sum = weigh(gate_rows, late_back)
    late_sum = lax.all_gather(late_sum, "section", axis=1, tiled=True)
    return combine(sections, place, gate_rows, proj_own, late_sum, returned)


def solution(mesh):
    return jax.shard_map(
        per_device,
        mesh=mesh,
        in_specs=(
            P(("dp", "expert"), None),
            P(("dp", "expert"), None),
            P(None, "section"),
            P("section", None),
            P("dp", "section"),
            P(("dp", "expert"), None),
            P(("dp", "expert"), None),
            P(("dp", "expert"), None, "section"),
            P(("dp", "expert"), None, "section"),
            P(("dp", "expert"), "section", None),
        ),
        out_specs=P(("dp", "expert"), "section"),
        check_vma=False,
    )
```

```python
import functools
import math

import jax
import jax.numpy as jnp
from jax import lax
from jax.experimental import pallas as pl
from jax.experimental.pallas import tpu as pltpu
from jax.sharding import PartitionSpec as P


D_VIT = 1152
HEADS = 16
TOP = 6
BF = jnp.bfloat16
F32 = jnp.float32

LATE = 128
VMEM = pl.BlockSpec(memory_space=pltpu.VMEM)
SMEM = pl.BlockSpec(memory_space=pltpu.SMEM)


def params(mib):
    return pltpu.CompilerParams(vmem_limit_bytes=mib * 2**20)


def dot(a, b):
    return jnp.dot(a, b, preferred_element_type=F32)


def dot_tn(a, b):
    return lax.dot_general(a, b, (((0,), (0,)), ((), ())), preferred_element_type=F32)


def dot_nt(a, b):
    return lax.dot_general(a, b, (((1,), (1,)), ((), ())), preferred_element_type=F32)


def shift(value, axis, step):
    count = lax.axis_size(axis)
    return lax.ppermute(value, axis, [(i, (i + step) % count) for i in range(count)])


def partner(value):
    count = lax.axis_size("dp")
    return lax.ppermute(value, "dp", [(i, i ^ 1) for i in range(count)])


def route_tables(routes, gates, expert_total, capacity):
    rows = routes.shape[0]
    ids = jnp.arange(expert_total, dtype=jnp.int32)
    named = routes[:, :, None] == ids[None, None, :]
    member = jnp.any(named, axis=1)
    weight = jnp.sum(jnp.where(named, gates[:, :, None], 0.0), axis=1)
    places = jnp.arange(rows, dtype=jnp.int32)
    before = (places[:, None] > places[None, :]).astype(BF)
    slot = dot(before, member.astype(BF))
    slot = jnp.where(member, slot, 255.0).astype(BF)
    lanes = jnp.arange(expert_total * capacity, dtype=jnp.int32)
    spread = (lanes[None, :] // capacity == ids[:, None]).astype(BF)
    hit = dot(slot, spread) == (lanes % capacity).astype(F32)[None, :]
    pick = dot_tn(spread, slot.T) == (lanes % capacity).astype(F32)[:, None]
    high = weight.astype(BF)
    low = (weight - high.astype(F32)).astype(BF)
    gate_high = jnp.where(hit, dot(high, spread), 0.0).astype(BF)
    gate_low = jnp.where(hit, dot(low, spread), 0.0).astype(BF)
    return pick.astype(BF), jnp.concatenate([gate_high, gate_low], axis=0)


def hbm(shape, dtype):
    return pltpu.MemorySpace.HBM(shape, dtype)


def keep(*values):
    return [pltpu.with_memory_space_constraint(v, pltpu.MemorySpace.HBM) for v in values]


def attend_body(head_dim, lengths, patches_hbm, w_hbm, out, patches, w, qkv, bias, heads, sems):
    rows = patches.shape[0]
    get_patches = pltpu.make_async_copy(patches_hbm, patches, sems.at[0])
    get_w = pltpu.make_async_copy(w_hbm, w, sems.at[1])
    get_patches.start()
    get_w.start()
    ends, end = [], 0
    for i in range(lengths.shape[1]):
        end = end + lengths[0, i] * 4
        ends.append(end)

    def image_of(axis):
        place = lax.broadcasted_iota(jnp.int32, (rows, 1) if axis == 0 else (1, rows), axis)
        return sum((place >= end).astype(jnp.int32) for end in ends)

    bias[...] = jnp.where(image_of(0) == image_of(1), 0.0, -1e30)
    get_patches.wait()
    values = patches[...].astype(F32)
    center = values - jnp.mean(values, axis=-1, keepdims=True)
    spread = jnp.mean(center * center, axis=-1, keepdims=True)
    patches[...] = (center * lax.rsqrt(spread + 1e-06)).astype(BF)
    get_w.wait()
    qkv[...] = dot_nt(w[...], patches[...])

    def one(h, carry):
        base = pl.multiple_of(h * 3 * head_dim, 8)
        query = (qkv[pl.ds(base, head_dim), :] * (1.0 / math.sqrt(head_dim))).astype(BF)
        key = qkv[pl.ds(base + head_dim, head_dim), :].astype(BF)
        value = qkv[pl.ds(base + 2 * head_dim, head_dim), :].astype(BF)
        scores = dot_tn(key, query) + bias[...]
        weights = jnp.exp(scores - jnp.max(scores, axis=0, keepdims=True))
        total = jnp.sum(weights, axis=0, keepdims=True)
        heads[pl.ds(pl.multiple_of(h * head_dim, 8), head_dim), :] = dot(value, weights.astype(BF)) / total
        return carry

    lax.fori_loop(0, w.shape[0] // (3 * head_dim), one, 0, unroll=4)
    out[...] = heads[...].astype(BF)


def attend(head_dim, lengths, patches, w):
    rows = patches.shape[0]
    features = w.shape[0]
    return pl.pallas_call(
        functools.partial(attend_body, head_dim),
        out_shape=hbm((features // 3, rows), BF),
        in_specs=[SMEM, pl.BlockSpec(memory_space=pl.ANY), pl.BlockSpec(memory_space=pl.ANY)],
        out_specs=VMEM,
        scratch_shapes=[
            pltpu.VMEM(patches.shape, BF),
            pltpu.VMEM(w.shape, BF),
            pltpu.VMEM((features, rows), F32),
            pltpu.VMEM((rows, rows), F32),
            pltpu.VMEM((features // 3, rows), F32),
            pltpu.SemaphoreType.DMA((2,)),
        ],
        compiler_params=params(24),
        name="attend",
    )(*keep(lengths, patches, w))


def project_body(place, patches, *refs):
    att, w_out, out_rows, out_other, rows, pick = refs[0:4], refs[4], refs[5:8], refs[8], refs[9:17], refs[17]
    own_out, late_out, slot_out = refs[18:21]
    att_v, out_v, proj_v, enc, sems = refs[21:]
    row_y, core = place[0], place[1]
    half = rows[0].shape[0]
    copies = []
    height = w_out.shape[0]
    for d in range(4):
        copies.append(pltpu.make_async_copy(att[d], att_v.at[pl.ds(d * height, height)], sems.at[d]))
    copies.append(pltpu.make_async_copy(w_out, out_v.at[pl.ds(0, height)], sems.at[4]))
    part = out_rows[0].shape[0]
    for d in (1, 2, 3):
        mine = pl.multiple_of(d * height + core * part, 16)
        other = pl.multiple_of(d * height + (1 - core) * part, 16)
        copies.append(pltpu.make_async_copy(out_rows[d - 1], out_v.at[pl.ds(mine, part)], sems.at[4 + d]))
        copies.append(
            pltpu.make_async_copy(out_other.at[pl.ds((d - 1) * part, part)], out_v.at[pl.ds(other, part)], sems.at[15 + d])
        )
    first = len(copies)
    for d in range(4):
        mine = pl.multiple_of(core * half, 64)
        other = pl.multiple_of((1 - core) * half, 64)
        copies.append(pltpu.make_async_copy(rows[d], proj_v.at[d, pl.ds(mine, half)], sems.at[8 + d]))
        copies.append(pltpu.make_async_copy(rows[4 + d], proj_v.at[d, pl.ds(other, half)], sems.at[12 + d]))
    for c in copies:
        c.start()
    for c in copies[:first]:
        c.wait()
    step = 128
    for r in range(patches.shape[0] // step):
        at = pl.ds(r * step, step)
        total = patches[at, :].astype(F32) + dot_tn(att_v[:, at], out_v[...])
        for q in range(enc.shape[0]):
            enc[q, at, :] = total[:, q * 128 : (q + 1) * 128]
    for c in copies[first:]:
        c.wait()
    merged = patches.shape[0] // 4
    acc = jnp.zeros(own_out.shape, F32)
    for d in range(4):
        j = lax.rem(row_y + 4 - d, 4)
        block = [enc[q, pl.ds(j, merged, stride=4), :].astype(BF) for q in range(enc.shape[0])]
        acc += dot(jnp.concatenate(block, axis=1), proj_v[d])
    own = acc.astype(BF)
    own_out[...] = own
    early = slot_out.shape[1]
    late_out[...] = own[:, early:]
    slot_out[...] = dot(pick[...], own[:, :early]).astype(BF)


def project(place, patches, att, w_out, out_rows, out_other, proj_rows, pick):
    merged = patches.shape[0] // 4
    columns = proj_rows[0].shape[1]
    half = proj_rows[0].shape[0]
    slots = pick.shape[0]
    anyspace = pl.BlockSpec(memory_space=pl.ANY)
    return pl.pallas_call(
        project_body,
        out_shape=(
            hbm((merged, columns), BF),
            jax.ShapeDtypeStruct((merged, LATE), BF),
            hbm((slots, columns - LATE), BF),
        ),
        in_specs=[SMEM, VMEM] + [anyspace] * 17 + [VMEM],
        out_specs=(VMEM, VMEM, VMEM),
        scratch_shapes=[
            pltpu.VMEM((4 * att[0].shape[0], att[0].shape[1]), BF),
            pltpu.VMEM((4 * w_out.shape[0], w_out.shape[1]), BF),
            pltpu.VMEM((4, 2 * half, columns), BF),
            pltpu.VMEM((patches.shape[1] // 128, patches.shape[0], 128), F32),
            pltpu.SemaphoreType.DMA((19,)),
        ],
        compiler_params=params(24),
        name="project",
    )(place, patches, *att, w_out, *out_rows, out_other, *proj_rows, pick)


def pick_body(pick, late, out):
    out[...] = dot(pick[...], late[...]).astype(BF)


def pick_rows(pick, late):
    return pl.pallas_call(
        pick_body,
        out_shape=hbm((pick.shape[0], late.shape[1]), BF),
        compiler_params=params(8),
        name="pick_rows",
    )(pick, late)


def squares(x):
    wide = x.astype(F32)
    wide = wide * wide
    return sum(wide[:, q * 128 : (q + 1) * 128] for q in range(x.shape[1] // 128))


ROWS = 384


def rows_spec(width, index=lambda r, *place: (r, 0)):
    return pl.BlockSpec((ROWS, width), index)


def lane_block(height, width, offset, sections):
    return pl.BlockSpec(
        (height, width), lambda r, place: (0, lax.rem(place[0] + offset, sections)), pipeline_mode=pl.Buffered(1)
    )


def whole_block(shape):
    return pl.BlockSpec(shape, lambda r, place: (0, 0), pipeline_mode=pl.Buffered(1))


def over_rows(body, rows, in_specs, out_specs, out_shape, operands):
    return pl.pallas_call(
        body,
        grid_spec=pltpu.PrefetchScalarGridSpec(
            num_scalar_prefetch=1, grid=(rows // ROWS,), in_specs=in_specs, out_specs=out_specs
        ),
        out_shape=out_shape,
        compiler_params=params(20),
    )(*operands)


def up_body(place, own, left, right, w_own, w_left, w_right, acc_out, square_out):
    width = own.shape[1]
    acc = jnp.zeros(acc_out.shape, F32)
    square = jnp.zeros(square_out.shape, F32)
    for piece, w in ((own, w_own), (left, w_left), (right, w_right)):
        x = piece[...]
        acc += dot_nt(x, w[:, :width])
        square += squares(x)
    acc_out[...] = acc
    square_out[...] = square


def up(columns, sections, place, own, left, right, w):
    rows, width = own.shape
    count = w.shape[0]
    return over_rows(
        up_body,
        rows,
        [rows_spec(width)] * 3 + [lane_block(count, columns, o, sections) for o in (0, 3, 1)],
        (rows_spec(count), rows_spec(128)),
        (hbm((rows, count), F32), hbm((rows, 128), F32)),
        (place, *keep(own, left, right, w, w, w)),
    )


def hidden_body(full, place, acc, square, late, far_a, far_b, w, w_late, w_down, down_late, *outs):
    hid_out, to_a, to_b, late_out = outs
    hidden_count = w_down.shape[0]
    width = far_a.shape[1]
    in_a = pl.program_id(0) < pl.num_programs(0) // 2
    x = jnp.where(in_a, far_a[...], far_b[...])
    y = late[...]
    total = acc[...] + dot_nt(x, w[:, :width])
    total += dot_nt(y, w_late[...])
    square_sum = square[...] + squares(x) + squares(y)
    mean = jnp.sum(square_sum, axis=-1, keepdims=True) * (1.0 / full)
    row_scale = lax.rsqrt(mean + 1e-06)
    gate = total[:, :hidden_count] * row_scale
    upper = total[:, hidden_count:] * row_scale
    hidden = (gate / (1.0 + jnp.exp(-gate)) * upper).astype(BF)
    hid_out[...] = hidden
    late_out[...] = dot(hidden, down_late[...]).astype(BF)
    part = dot(hidden, w_down[:, :width]).astype(BF)

    @pl.when(in_a)
    def _():
        to_a[...] = part

    @pl.when(jnp.logical_not(in_a))
    def _():
        to_b[...] = part


def hidden_units(columns, sections, place, acc, square, late, far_a, far_b, w, w_late, w_down, down_late):
    rows, width = acc.shape[0], far_a.shape[1]
    half = rows // 2 // ROWS
    spec_a = rows_spec(width, lambda r, place: (jnp.minimum(r, half - 1), 0))
    spec_b = rows_spec(width, lambda r, place: (jnp.maximum(r - half, 0), 0))
    return over_rows(
        functools.partial(hidden_body, columns * sections),
        rows,
        [rows_spec(acc.shape[1]), rows_spec(128), rows_spec(late.shape[1]), spec_a, spec_b]
        + [lane_block(w.shape[0], columns, 2, sections), whole_block(w_late.shape)]
        + [lane_block(w_down.shape[0], columns, 2, sections), whole_block(down_late.shape)],
        (rows_spec(w_down.shape[0]), spec_a, spec_b, rows_spec(late.shape[1])),
        (hbm((rows, w_down.shape[0]), BF), *[hbm((rows // 2, width), BF)] * 2, hbm(late.shape, BF)),
        (place, *keep(acc, square), late, *keep(far_a, far_b, w, w_late, w_down, down_late)),
    )


def down_body(count, place, hidden, *refs):
    h = hidden[...]
    for w, out in zip(refs[:count], refs[count:]):
        out[...] = dot(h, w[:, : out.shape[1]]).astype(BF)


def down(columns, sections, offsets, place, hidden, w, width):
    rows, height = hidden.shape
    count = len(offsets)
    blocks = [lane_block(height, columns, o, sections) for o in offsets]
    return over_rows(
        functools.partial(down_body, count),
        rows,
        [rows_spec(height)] + blocks,
        [rows_spec(width)] * count,
        [hbm((rows, width), BF)] * count,
        (place, *keep(hidden, *[w] * count)),
    )


def cut_body(left, right, top, bottom):
    top[...] = left[...]
    bottom[...] = right[...]


def cut(left, right):
    rows, width = left.shape
    half = rows // 2 // ROWS
    return pl.pallas_call(
        cut_body,
        out_shape=(hbm((rows // 2, width), BF),) * 2,
        grid=(half,),
        in_specs=[rows_spec(width), rows_spec(width, lambda r: (r + half, 0))],
        out_specs=[rows_spec(width)] * 2,
        compiler_params=params(8),
        name="cut",
    )(*keep(left, right))


def add_body(right, left, via_a, via_b, right_out, left_out):
    right_out[...] = (right[...].astype(F32) + via_a[...].astype(F32)).astype(BF)
    left_out[...] = (left[...].astype(F32) + via_b[...].astype(F32)).astype(BF)


def add(right, left, via_a, via_b):
    rows, width = right.shape
    half = rows // 2 // ROWS
    whole = [rows_spec(width), rows_spec(width, lambda r: (r + half, 0))]
    return pl.pallas_call(
        add_body,
        out_shape=(hbm(right.shape, BF), hbm(left.shape, BF)),
        grid=(half,),
        in_specs=whole + [rows_spec(width)] * 2,
        out_specs=whole,
        input_output_aliases={0: 0, 1: 1},
        compiler_params=params(8),
        name="add",
    )(*keep(right, left), via_a, via_b)


def weigh_body(gates, late, out):
    both = dot(gates[...], late[...])
    merged = both.shape[0] // 2
    out[...] = (both[:merged] + both[merged:]).astype(BF)


def weigh(gates, late):
    return pl.pallas_call(
        weigh_body,
        out_shape=jax.ShapeDtypeStruct((gates.shape[0] // 2, late.shape[1]), BF),
        compiler_params=params(12),
        name="weigh",
    )(gates, late)


def settle_body(sections, place, own, late, out):
    width = own.shape[1] - LATE
    out[:, :width] = own[:, :width].astype(F32)
    total = own[:, width:].astype(F32)
    for s in range(sections):
        first = s * sections * LATE + place[0] * LATE
        total += late[:, pl.ds(pl.multiple_of(first, LATE), LATE)].astype(F32)
    out[:, width:] = total


def settle(sections, place, own, late):
    return pl.pallas_call(
        functools.partial(settle_body, sections),
        out_shape=jax.ShapeDtypeStruct(own.shape, F32),
        in_specs=[SMEM, VMEM, VMEM],
        out_specs=VMEM,
        compiler_params=params(12),
        name="settle",
    )(place, own, late)


def combine_body(gates, early, base, out):
    merged, width = out.shape[0], early.shape[1]
    both = dot(gates[...], early[...])
    out[:, :width] = (base[:, :width] + both[:merged] + both[merged:]).astype(BF)
    out[:, width:] = base[:, width:].astype(BF)


def combine(gates, early, base):
    return pl.pallas_call(
        combine_body,
        out_shape=jax.ShapeDtypeStruct(base.shape, BF),
        compiler_params=params(12),
        name="combine",
    )(gates, early, base)


def per_device(patches, lengths, w_qkv, w_out, w_proj, routes, gates, w_gate, w_up, w_down):
    data_count = lax.axis_size("dp")
    owner_count = lax.axis_size("expert")
    sections = lax.axis_size("section")
    merged_count = patches.shape[0] // 4
    expert_total = data_count * owner_count
    capacity = max(2, min(merged_count, 2 * merged_count * TOP // expert_total))
    columns = w_proj.shape[1]
    early = columns - LATE
    place = jnp.stack([lax.axis_index("section")]).astype(jnp.int32)
    dp_place = jnp.stack([lax.axis_index("dp") // 2, lax.axis_index("dp") % 2]).astype(jnp.int32)

    out_rows, mine = [], [w_proj]
    out_half = lax.dynamic_slice_in_dim(w_out, dp_place[1] * (w_out.shape[0] // 2), w_out.shape[0] // 2, axis=0)
    for d in (1, 2, 3):
        mine.append(shift(w_proj, "dp", 2 * d))
        out_rows.append(shift(out_half, "section", d))
    proj_rows = mine + [partner(m) for m in mine]
    out_other = partner(jnp.concatenate(out_rows, axis=0))

    attended = attend(D_VIT // HEADS, lengths, patches, w_qkv.T)

    att = [attended]
    for d in (1, 2, 3):
        att.append(shift(attended, "section", d))
    pick, gate_rows = route_tables(routes, gates, expert_total, capacity)
    w_both = jnp.concatenate([w_gate[0].T, w_up[0].T], axis=0)
    last = lambda w: jnp.concatenate([w[:, s * columns + early : (s + 1) * columns] for s in range(sections)], axis=1)
    w_late, down_late = last(w_both), last(w_down[0])
    proj_own, late, outgoing = project(dp_place, patches, att, w_out, out_rows, out_other, proj_rows, pick)

    def exchange(value):
        wide = value.reshape(expert_total, capacity, value.shape[1])
        wide = lax.all_to_all(wide, ("dp", "expert"), split_axis=0, concat_axis=0, tiled=True)
        return wide.reshape(value.shape)

    own = exchange(outgoing)
    late_all = lax.all_gather(late, "section", axis=1, tiled=True)
    late_rows = pick_rows(pick, late_all)
    late_rows = exchange(late_rows)
    left = shift(own, "section", 1)
    right = shift(own, "section", -1)
    top, bottom = cut(left, right)
    far_a = shift(top, "section", 1)
    far_b = shift(bottom, "section", -1)
    acc, square = up(columns, sections, place, own, left, right, w_both)
    hidden, to_a, to_b, late_out = hidden_units(
        columns, sections, place, acc, square, late_rows, far_a, far_b, w_both, w_late, w_down[0], down_late
    )
    via_a = shift(to_a, "section", 1)
    via_b = shift(to_b, "section", -1)
    late_back = exchange(late_out)
    to_right, to_left, here = down(columns, sections, (1, 3, 0), place, hidden, w_down[0], early)
    to_right, to_left = add(to_right, to_left, via_a, via_b)
    from_left = shift(to_right, "section", 1)
    from_right = shift(to_left, "section", -1)
    total = (here.astype(F32) + from_left.astype(F32) + from_right.astype(F32)).astype(BF)
    returned = exchange(total)
    late_sum = weigh(gate_rows, late_back)
    late_sum = lax.all_gather(late_sum, "section", axis=1, tiled=True)
    base = settle(sections, place, proj_own, late_sum)
    return combine(gate_rows, returned, base)


def solution(mesh):
    return jax.shard_map(
        per_device,
        mesh=mesh,
        in_specs=(
            P(("dp", "expert"), None),
            P(("dp", "expert"), None),
            P(None, "section"),
            P("section", None),
            P("dp", "section"),
            P(("dp", "expert"), None),
            P(("dp", "expert"), None),
            P(("dp", "expert"), None, "section"),
            P(("dp", "expert"), None, "section"),
            P(("dp", "expert"), "section", None),
        ),
        out_specs=P(("dp", "expert"), "section"),
        check_vma=False,
    )
```
